32 devices in a mesh: fsdp: 8 (over y, x, core), replica: 4 (over z).
Axes of the slice: x: 2, y: 2, z: 4, core: 2. Of those that a mesh axis runs over, the one named last changes fastest.
Arguments:
- inputs: bfloat16 [8, 512, 768], P('fsdp', 'replica'), may hold values from -6 to 6
- cotangent: bfloat16 [8, 512, 768], P('fsdp', 'replica'), may hold values from -6 to 6
- segments: int32 [8, 512], P('fsdp'), may hold values from 0 to 2, never falling along the last dimension, each value on 1 to 256 neighbouring positions
- w_qkv_state: float32 [3, 768, 2304], P(None, 'fsdp'), as said below
- b_qkv_state: float32 [3, 2, 768], P(None, None, 'fsdp')
- w_o_state: float32 [3, 768, 768], P(None, 'fsdp')
- w_fc_state: float32 [3, 768, 3072], P(None, 'fsdp')
- b_fc_state: float32 [3, 3072], P(None, 'fsdp')
- w_pr_state: float32 [3, 3072, 768], P(None, 'fsdp')
- vec_state: float32 [3, 6, 768], P(None, None, 'fsdp'), as said below
Outputs:
- outputs: bfloat16 [8, 512, 768], P('fsdp', 'replica')
- input_grad: bfloat16 [8, 512, 768], P('fsdp', 'replica')
- grad_w_qkv: float32 [768, 2304], P('fsdp')
- grad_b_qkv: float32 [2, 768], P(None, 'fsdp')
- grad_w_o: float32 [768, 768], P('fsdp')
- grad_w_fc: float32 [768, 3072], P('fsdp')
- grad_b_fc: float32 [3072], P('fsdp')
- grad_w_pr: float32 [3072, 768], P('fsdp')
- grad_vectors: float32 [6, 768], P(None, 'fsdp')
- new_w_qkv: float32 [3, 768, 2304], P(None, 'fsdp')
- new_b_qkv: float32 [3, 2, 768], P(None, None, 'fsdp')
- new_w_o: float32 [3, 768, 768], P(None, 'fsdp')
- new_w_fc: float32 [3, 768, 3072], P(None, 'fsdp')
- new_b_fc: float32 [3, 3072], P(None, 'fsdp')
- new_w_pr: float32 [3, 3072, 768], P(None, 'fsdp')
- new_vectors: float32 [3, 6, 768], P(None, None, 'fsdp')
The draws below stay inside these ranges and needn't reach their ends.
Inputs may be any that keep to these rules, and one draw needn't show every extreme that they name: `w_qkv_state`: slice 0 of each state is the parameter, slice 1 its first moment, slice 2 its second moment, which is positive. `vec_state`: as for w_qkv_state.
All inputs are finite; a program needn't handle non-finite values.
Results may differ from the reference program's by a relative error of at most 0.012.
Values may be sent and summed in bfloat16 or wider, within the bound.
A program may use at most 192 MiB of HBM per device.

```python
import math
import jax
import jax.numpy as jnp
import numpy as np
from jax import lax

D = 768
H = 12
HD = 64
FF = 3072
LENGTH = 512
STEP = 2
SEQS = 8
TOKENS = 4096


def spread(key, shape):
    return jax.random.normal(key, shape, jnp.float32)


def with_moments(key, shape, weight):
    key_first, key_second = jax.random.split(jax.random.fold_in(key, 97))
    first = 0.05 * jax.random.normal(key_first, shape, jnp.float32)
    second = jnp.exp(jax.random.uniform(key_second, shape, jnp.float32, math.log(0.001), math.log(0.05)))
    return jnp.stack([weight, first, second])


def draw_w_qkv_state(key, part):
    keys = jax.random.split(jax.random.fold_in(key, 11), 5)
    weight = spread(keys[0], (D, 3 * D)) / math.sqrt(D)
    return with_moments(keys[4], (D, 3 * D), weight)


def draw_b_qkv_state(key, part):
    keys = jax.random.split(jax.random.fold_in(key, 12), 2)
    return with_moments(keys[1], (2, D), 0.3 * spread(keys[0], (2, D)))


def draw_w_o_state(key, part):
    keys = jax.random.split(jax.random.fold_in(key, 13), 2)
    return with_moments(keys[1], (D, D), spread(keys[0], (D, D)) / math.sqrt(D // 16))


def draw_w_fc_state(key, part):
    keys = jax.random.split(jax.random.fold_in(key, 14), 2)
    return with_moments(keys[1], (D, FF), spread(keys[0], (D, FF)) / math.sqrt(D))


def draw_b_fc_state(key, part):
    keys = jax.random.split(jax.random.fold_in(key, 15), 2)
    return with_moments(keys[1], (FF,), 0.3 * spread(keys[0], (FF,)))


def draw_w_pr_state(key, part):
    keys = jax.random.split(jax.random.fold_in(key, 16), 2)
    return with_moments(keys[1], (FF, D), spread(keys[0], (FF, D)) / math.sqrt(FF))


def draw_vec_state(key, part):
    keys = jax.random.split(jax.random.fold_in(key, 17), 2)
    raw = spread(keys[0], (6, D))
    gain_rows = jnp.array([1.0, 0.0, 0.0, 1.0, 0.0, 0.0], jnp.float32)[:, None]
    weight = gain_rows * (1.0 + 0.1 * raw) + (1.0 - gain_rows) * 0.3 * raw
    return with_moments(keys[1], (6, D), weight)


def raised(values, key, source, target, parts, factor):
    owner, partner = [(jnp.arange(values.shape[axis_at]) // (values.shape[axis_at] // parts)).reshape([-1 if axis == axis_at else 1 for axis in range(values.ndim)]) for axis_at in (source, target)]
    chosen = jax.random.permutation(key, parts)[partner]
    strong = (owner == chosen) | (owner == (partner + parts // 2) % parts)
    return jnp.where(strong, factor * values, values)


def block_scale(key, dims, cuts, smallest, high):
    def one(axis_at, parts):
        draws = jax.random.uniform(jax.random.fold_in(jax.random.fold_in(key, 6), axis_at), (parts,), jnp.float32, smallest / len(cuts), high / len(cuts))
        return jnp.repeat(jnp.exp(draws), dims[axis_at] // parts).reshape((-1,) + (1,) * (len(dims) - axis_at - 1))

    factor_of = one(*cuts[0])
    for cut in cuts[1:]:
        factor_of = factor_of * one(*cut)
    return factor_of


def split_up(amount, total, bound, skew):
    portions = [(1 << 20) // math.isqrt(grade ** skew) + 1 for grade in range(2, amount + 1)]
    surplus, holding = total - bound - (amount - 1), [1] * (amount - 1)
    while surplus > 0:
        candidates = [i for i in range(amount - 1) if holding[i] < bound]
        whole, left = sum([portions[i] for i in candidates]), surplus
        for i in candidates:
            addition = min(bound - holding[i], max(1, left * portions[i] // whole), surplus)
            holding[i] = holding[i] + addition
            surplus = surplus - addition
    return np.array([bound] + holding)


def ragged(rng, count, total, most, skew):
    if count == 2:
        one = jax.random.randint(rng, (), max(1, total - most), min(most, total - 1) + 1)
        return jnp.stack([one, total - one])
    sizes = jnp.asarray(split_up(count, total, most, skew), jnp.int32)
    pairs = (count - 1) // 2
    donor, taker = sizes[1:1 + 2 * pairs:2], sizes[2:2 + 2 * pairs:2]
    slack = jnp.minimum(donor - 1, most - taker)
    passed = jax.random.randint(jax.random.fold_in(rng, 1), (pairs,), 0, 1 << 20) % (slack + 1)
    sizes = sizes.at[1:1 + 2 * pairs:2].set(donor - passed).at[2:2 + 2 * pairs:2].set(taker + passed)
    return sizes[jax.random.permutation(jax.random.fold_in(rng, 2), count)]


def gaussian(rng, shape, deviation, most, pieces=(), held_as=jnp.bfloat16):
    gain = block_scale(rng, shape, pieces, -0.22, 0.18) if pieces else 1.0
    values = jax.random.normal(rng, shape, jnp.float32) * deviation * gain
    return jnp.minimum(jnp.maximum(values, -most), most).astype(held_as)


def bell_draw_with(stream_key, dims, deviation, most, cuts, heavy, kind=jnp.bfloat16):
    values = deviation * jax.random.normal(stream_key, dims, jnp.float32)
    if cuts:
        values = values * block_scale(stream_key, dims, cuts, -0.22, 0.18)
    return jnp.clip(raised(values, jax.random.fold_in(stream_key, 3), *heavy), -most, most).astype(kind)


def setup_inputs(seed: int = 0) -> dict:
    seeds = jax.random.split(jax.random.key(seed), 11)
    inputs = gaussian(seeds[0], (SEQS, LENGTH, D), 1.0, 6.0, ((0, 8), (1, 4)))
    cotangent = bell_draw_with(seeds[1], (SEQS, LENGTH, D), 1.0, 6.0, ((0, 8), (1, 4)), (0, 2, 8, 2.0))
    segments = jax.vmap(lambda own: jnp.searchsorted(jnp.cumsum(ragged(own, 3, LENGTH, LENGTH // 2, 0)), jnp.arange(LENGTH), side="right"))(jax.random.split(seeds[2], SEQS)).reshape((SEQS, LENGTH)).astype(jnp.int32)
    w_qkv_state = draw_w_qkv_state(jax.random.fold_in(seeds[10], 71), 0)
    b_qkv_state = draw_b_qkv_state(jax.random.fold_in(seeds[10], 71), 0)
    w_o_state = draw_w_o_state(jax.random.fold_in(seeds[10], 71), 0)
    w_fc_state = draw_w_fc_state(jax.random.fold_in(seeds[10], 71), 0)
    b_fc_state = draw_b_fc_state(jax.random.fold_in(seeds[10], 71), 0)
    w_pr_state = draw_w_pr_state(jax.random.fold_in(seeds[10], 71), 0)
    vec_state = draw_vec_state(jax.random.fold_in(seeds[10], 71), 0)
    return dict(inputs=inputs, cotangent=cotangent, segments=segments, w_qkv_state=w_qkv_state, b_qkv_state=b_qkv_state, w_o_state=w_o_state, w_fc_state=w_fc_state, b_fc_state=b_fc_state, w_pr_state=w_pr_state, vec_state=vec_state)


NORM_EPSILON = 1e-05
ADAM_EPSILON = 1e-08
BETA_FIRST = 0.9
BETA_SECOND = 0.95
LEARN_RATE = 0.06
WEIGHT_DECAY = 0.1
GELU_SCALE = math.sqrt(2.0 / math.pi)
SCORE_SCALE = 0.125

def layer_norm(values, norm_gain, norm_bias):
    center = values - lax.optimization_barrier(jnp.mean(values, -1, keepdims=True))
    scaler = lax.rsqrt(lax.optimization_barrier(jnp.mean(center * center, -1, keepdims=True)) + NORM_EPSILON)
    normed = center * scaler
    return (normed * norm_gain + norm_bias, normed, scaler)

def norm_back(grad_out, norm_gain, normed, scaler):
    scaled = grad_out * norm_gain
    return scaler * (scaled - lax.optimization_barrier(jnp.mean(scaled, -1, keepdims=True)) - normed * lax.optimization_barrier(jnp.mean(scaled * normed, -1, keepdims=True)))

def gelu_parts(pre_act):
    inner = GELU_SCALE * (pre_act + 0.044715 * pre_act * pre_act * pre_act)
    tangent = jnp.tanh(inner)
    activ = 0.5 * pre_act * (1.0 + tangent)
    slope = 0.5 * (1.0 + tangent) + 0.5 * pre_act * (1.0 - tangent * tangent) * GELU_SCALE * (1.0 + 3.0 * 0.044715 * pre_act * pre_act)
    return (activ, slope)

def rounded_float(values):
    return lax.optimization_barrier(values.astype(jnp.bfloat16)).astype(jnp.float32)

def adamw(state, grad, decay):
    first = BETA_FIRST * state[1] + (1.0 - BETA_FIRST) * grad
    second = BETA_SECOND * state[2] + (1.0 - BETA_SECOND) * grad * grad
    first_hat = first / (1.0 - BETA_FIRST ** STEP)
    second_hat = second / (1.0 - BETA_SECOND ** STEP)
    weight = state[0] - LEARN_RATE * (first_hat / (jnp.sqrt(second_hat) + ADAM_EPSILON) + decay * state[0])
    return jnp.stack([weight, first, second])

def reference(inputs, cotangent, segments, w_qkv_state, b_qkv_state, w_o_state, w_fc_state, b_fc_state, w_pr_state, vec_state):
    w_qkv = w_qkv_state[0].astype(jnp.bfloat16)
    w_out = w_o_state[0].astype(jnp.bfloat16)
    w_fc = w_fc_state[0].astype(jnp.bfloat16)
    w_pr = w_pr_state[0].astype(jnp.bfloat16)
    b_qkv = rounded_float(b_qkv_state[0])
    bias_row = jnp.concatenate([b_qkv[0], jnp.zeros((D,), jnp.float32), b_qkv[1]])
    b_fc = rounded_float(b_fc_state[0])
    vectors = rounded_float(vec_state[0])
    positions = jnp.arange(LENGTH, dtype=jnp.int32)

    def one_sequence(totals, element):
        tokens_in, cot_in, seg_row = element
        hidden = tokens_in.astype(jnp.float32)
        attn_in_f, normed_one, scale_one = layer_norm(hidden, vectors[0], vectors[1])
        attn_in = attn_in_f.astype(jnp.bfloat16)
        projected = (jnp.dot(attn_in, w_qkv, preferred_element_type=jnp.float32) + bias_row).astype(jnp.bfloat16)
        query_h = projected[:, :D].astype(jnp.float32).reshape(LENGTH, H, HD)
        key_h = projected[:, D:2 * D].astype(jnp.float32).reshape(LENGTH, H, HD)
        value_h = projected[:, 2 * D:].astype(jnp.float32).reshape(LENGTH, H, HD)
        allowed = (seg_row[:, None] == seg_row[None, :]) & (positions[None, :] <= positions[:, None])
        scores = jnp.einsum('qhd,khd->hqk', query_h, key_h) * SCORE_SCALE
        scores = jnp.where(allowed[None], scores, -1e+30)
        top = lax.optimization_barrier(jnp.max(scores, -1, keepdims=True))
        log_norm = top + jnp.log(lax.optimization_barrier(jnp.sum(jnp.exp(scores - top), -1, keepdims=True)))
        prob_f = jnp.exp(scores - log_norm)
        prob = prob_f.astype(jnp.bfloat16).astype(jnp.float32)
        attended = jnp.einsum('hqk,khd->qhd', prob, value_h).reshape(LENGTH, D).astype(jnp.bfloat16)
        mixed = hidden + jnp.dot(attended, w_out, preferred_element_type=jnp.float32) + vectors[2]
        ffn_in_f, normed_two, scale_two = layer_norm(mixed, vectors[3], vectors[4])
        ffn_in = ffn_in_f.astype(jnp.bfloat16)
        pre_act = jnp.dot(ffn_in, w_fc, preferred_element_type=jnp.float32) + b_fc
        activ, slope = gelu_parts(pre_act)
        activ_b = activ.astype(jnp.bfloat16)
        result = mixed + jnp.dot(activ_b, w_pr, preferred_element_type=jnp.float32) + vectors[5]
        cot_f = cot_in.astype(jnp.float32)
        grad_w_pr = jnp.dot(activ_b.T, cot_in, preferred_element_type=jnp.float32)
        grad_b_pr = lax.optimization_barrier(jnp.sum(cot_f, 0))
        grad_pre = jnp.dot(cot_in, w_pr.T, preferred_element_type=jnp.float32) * slope
        grad_pre_b = grad_pre.astype(jnp.bfloat16)
        grad_w_fc = jnp.dot(ffn_in.T, grad_pre_b, preferred_element_type=jnp.float32)
        grad_b_fc = lax.optimization_barrier(jnp.sum(grad_pre, 0))
        grad_ffn = jnp.dot(grad_pre_b, w_fc.T, preferred_element_type=jnp.float32)
        grad_gain_two = lax.optimization_barrier(jnp.sum(grad_ffn * normed_two, 0))
        grad_bias_two = lax.optimization_barrier(jnp.sum(grad_ffn, 0))
        grad_mixed = cot_f + norm_back(grad_ffn, vectors[3], normed_two, scale_two)
        grad_mixed_b = grad_mixed.astype(jnp.bfloat16)
        grad_w_out = jnp.dot(attended.T, grad_mixed_b, preferred_element_type=jnp.float32)
        grad_b_out = lax.optimization_barrier(jnp.sum(grad_mixed, 0))
        grad_att = jnp.dot(grad_mixed_b, w_out.T, preferred_element_type=jnp.float32).astype(jnp.bfloat16)
        grad_att_h = grad_att.astype(jnp.float32).reshape(LENGTH, H, HD)
        delta = jnp.einsum('qhd,qhd->hq', grad_att_h, attended.astype(jnp.float32).reshape(LENGTH, H, HD))[..., None]
        grad_prob = jnp.einsum('qhd,khd->hqk', grad_att_h, value_h)
        grad_score = (prob_f * (grad_prob - delta) * SCORE_SCALE).astype(jnp.bfloat16).astype(jnp.float32)
        grad_query = jnp.einsum('hqk,khd->qhd', grad_score, key_h).reshape(LENGTH, D)
        grad_key = jnp.einsum('hqk,qhd->khd', grad_score, query_h).reshape(LENGTH, D)
        grad_value = jnp.einsum('hqk,qhd->khd', prob, grad_att_h).reshape(LENGTH, D)
        grad_proj = jnp.concatenate([grad_query, grad_key, grad_value], 1)
        grad_proj_b = grad_proj.astype(jnp.bfloat16)
        grad_w_qkv = jnp.dot(attn_in.T, grad_proj_b, preferred_element_type=jnp.float32)
        grad_b_qkv = jnp.stack([lax.optimization_barrier(jnp.sum(grad_query, 0)), lax.optimization_barrier(jnp.sum(grad_value, 0))])
        grad_in = jnp.dot(grad_proj_b, w_qkv.T, preferred_element_type=jnp.float32)
        grad_gain_one = lax.optimization_barrier(jnp.sum(grad_in * normed_one, 0))
        grad_bias_one = lax.optimization_barrier(jnp.sum(grad_in, 0))
        grad_input = grad_mixed + norm_back(grad_in, vectors[0], normed_one, scale_one)
        grad_vec = jnp.stack([grad_gain_one, grad_bias_one, grad_b_out, grad_gain_two, grad_bias_two, grad_b_pr])
        grads = (grad_w_qkv, grad_b_qkv, grad_w_out, grad_w_fc, grad_b_fc, grad_w_pr, grad_vec)
        totals = jax.tree.map(jnp.add, totals, grads)
        return (totals, (result.astype(jnp.bfloat16), grad_input.astype(jnp.bfloat16)))
    start = (jnp.zeros((D, 3 * D), jnp.float32), jnp.zeros((2, D), jnp.float32), jnp.zeros((D, D), jnp.float32), jnp.zeros((D, FF), jnp.float32), jnp.zeros((FF,), jnp.float32), jnp.zeros((FF, D), jnp.float32), jnp.zeros((6, D), jnp.float32))
    totals, stacked = lax.scan(one_sequence, start, (inputs, cotangent, segments))
    factor = float(TOKENS) ** (-0.5)
    grads = [total * factor for total in totals]
    new_w_qkv = adamw(w_qkv_state, grads[0], WEIGHT_DECAY)
    new_b_qkv = adamw(b_qkv_state, grads[1], 0.0)
    new_w_o = adamw(w_o_state, grads[2], WEIGHT_DECAY)
    new_w_fc = adamw(w_fc_state, grads[3], WEIGHT_DECAY)
    new_b_fc = adamw(b_fc_state, grads[4], 0.0)
    new_w_pr = adamw(w_pr_state, grads[5], WEIGHT_DECAY)
    new_vectors = adamw(vec_state, grads[6], 0.0)
    return (stacked[0], stacked[1], grads[0], grads[1], grads[2], grads[3], grads[4], grads[5], grads[6], new_w_qkv, new_b_qkv, new_w_o, new_w_fc, new_b_fc, new_w_pr, new_vectors)
```

```python
import math

import jax
import jax.numpy as jnp
from jax import lax
from jax.sharding import PartitionSpec as P

HD = 64
STEP = 2


NORM_EPSILON = 1e-05
ADAM_EPSILON = 1e-08
BETA_FIRST = 0.9
BETA_SECOND = 0.95
LEARN_RATE = 0.06
WEIGHT_DECAY = 0.1
GELU_SCALE = math.sqrt(2.0 / math.pi)
SCORE_SCALE = 0.125


def layer_norm(values, norm_gain, norm_bias):
    center = values - jnp.mean(values, -1, keepdims=True)
    scaler = lax.rsqrt(jnp.mean(center * center, -1, keepdims=True) + NORM_EPSILON)
    normed = center * scaler
    return (normed * norm_gain + norm_bias, normed, scaler)


def norm_back(grad_out, norm_gain, normed, scaler):
    scaled = grad_out * norm_gain
    return scaler * (
        scaled
        - jnp.mean(scaled, -1, keepdims=True)
        - normed * jnp.mean(scaled * normed, -1, keepdims=True)
    )


def gelu_parts(pre_act):
    inner = GELU_SCALE * (pre_act + 0.044715 * pre_act * pre_act * pre_act)
    tangent = jnp.tanh(inner)
    activ = 0.5 * pre_act * (1.0 + tangent)
    slope = 0.5 * (1.0 + tangent) + 0.5 * pre_act * (1.0 - tangent * tangent) * GELU_SCALE * (
        1.0 + 3.0 * 0.044715 * pre_act * pre_act
    )
    return (activ, slope)


def adamw(state, grad, decay):
    first = BETA_FIRST * state[1] + (1.0 - BETA_FIRST) * grad
    second = BETA_SECOND * state[2] + (1.0 - BETA_SECOND) * grad * grad
    first_hat = first / (1.0 - BETA_FIRST**STEP)
    second_hat = second / (1.0 - BETA_SECOND**STEP)
    weight = state[0] - LEARN_RATE * (
        first_hat / (jnp.sqrt(second_hat) + ADAM_EPSILON) + decay * state[0]
    )
    return jnp.stack([weight, first, second])


def split_heads(query, key_value):
    width = query.shape[1]
    heads = width // HD
    query_h = query.reshape(query.shape[0], heads, HD)
    key_h = key_value[:, :width].reshape(key_value.shape[0], heads, HD)
    value_h = key_value[:, width:].reshape(key_value.shape[0], heads, HD)
    return (query_h, key_h, value_h)


def masked_scores(query_h, key_h, seg_query, seg_key, pos_query, pos_key):
    allowed = (seg_query[:, None] == seg_key[None, :]) & (pos_key[None, :] <= pos_query[:, None])
    scores = (
        jnp.einsum("qhd,khd->hqk", query_h, key_h, preferred_element_type=jnp.float32) * SCORE_SCALE
    )
    return jnp.where(allowed[None], scores, -1e30)


def attend_forward(query, key_value, seg_query, seg_key, pos_query, pos_key):
    query_h, key_h, value_h = split_heads(query, key_value)
    scores = masked_scores(query_h, key_h, seg_query, seg_key, pos_query, pos_key)
    top = jnp.max(scores, -1, keepdims=True)
    log_norm = top + jnp.log(jnp.sum(jnp.exp(scores - top), -1, keepdims=True))
    prob = jnp.exp(scores - log_norm).astype(jnp.bfloat16)
    attended = jnp.einsum("hqk,khd->qhd", prob, value_h, preferred_element_type=jnp.float32)
    return (attended.reshape(query.shape[0], query.shape[1]).astype(jnp.bfloat16), log_norm)


def attend_backward(
    query, key_value, seg_query, seg_key, pos_query, pos_key, log_norm, attended, grad_att
):
    query_h, key_h, value_h = split_heads(query, key_value)
    rows = query.shape[0]
    heads = query_h.shape[1]
    scores = masked_scores(query_h, key_h, seg_query, seg_key, pos_query, pos_key)
    prob_f = jnp.exp(scores - log_norm)
    prob = prob_f.astype(jnp.bfloat16)
    grad_att_h = grad_att.reshape(rows, heads, HD)
    delta = jnp.sum(
        grad_att_h.astype(jnp.float32) * attended.reshape(rows, heads, HD).astype(jnp.float32), -1
    )
    grad_prob = jnp.einsum("qhd,khd->hqk", grad_att_h, value_h, preferred_element_type=jnp.float32)
    grad_score = (prob_f * (grad_prob - delta.T[..., None]) * SCORE_SCALE).astype(jnp.bfloat16)
    grad_query = jnp.einsum("hqk,khd->qhd", grad_score, key_h, preferred_element_type=jnp.float32)
    grad_key = jnp.einsum("hqk,qhd->khd", grad_score, query_h, preferred_element_type=jnp.float32)
    grad_value = jnp.einsum("hqk,qhd->khd", prob, grad_att_h, preferred_element_type=jnp.float32)
    key_rows = key_value.shape[0]
    grad_kv = jnp.concatenate([grad_key.reshape(key_rows, -1), grad_value.reshape(key_rows, -1)], 1)
    return (grad_query.reshape(rows, -1), grad_kv)


def map_sequences(function, elements):
    if elements[0].shape[0] == 1:
        return jax.tree.map(lambda x: x[None], function([x[0] for x in elements]))
    return lax.map(function, elements)


def reduce_matrix(grad):
    part = lax.psum_scatter(grad.astype(jnp.bfloat16), "fsdp", scatter_dimension=0, tiled=True)
    part = lax.psum_scatter(part, "replica", scatter_dimension=1, tiled=True)
    return lax.all_gather(part, "replica", axis=1, tiled=True).astype(jnp.float32)


def body(
    inputs,
    cotangent,
    segments,
    w_qkv_state,
    b_qkv_state,
    w_o_state,
    w_fc_state,
    b_fc_state,
    w_pr_state,
    vec_state,
):
    shard = vec_state.shape[2]
    hidden_ratio = b_fc_state.shape[1] // shard
    small = jnp.concatenate(
        [vec_state[0], b_qkv_state[0], b_fc_state[0].reshape(hidden_ratio, shard)], 0
    ).astype(jnp.bfloat16)
    small_all = lax.all_gather(small, "fsdp", axis=0, tiled=False)
    w_qkv = lax.all_gather(w_qkv_state[0].astype(jnp.bfloat16), "fsdp", axis=0, tiled=True)
    w_out = lax.all_gather(w_o_state[0].astype(jnp.bfloat16), "fsdp", axis=0, tiled=True)
    w_fc = lax.all_gather(w_fc_state[0].astype(jnp.bfloat16), "fsdp", axis=0, tiled=True)
    w_pr = lax.all_gather(w_pr_state[0].astype(jnp.bfloat16), "fsdp", axis=0, tiled=True)
    vectors = small_all[:, :6].transpose(1, 0, 2).reshape(6, -1)
    b_qkv = small_all[:, 6:8].transpose(1, 0, 2).reshape(2, -1)
    b_fc = small_all[:, 8:].reshape(-1)
    vector_f = vectors.astype(jnp.float32)
    bias_row = jnp.concatenate([b_qkv[0], jnp.zeros_like(b_qkv[0]), b_qkv[1]]).astype(jnp.float32)
    seq_count, span, width = inputs.shape
    full_len = segments.shape[1]
    row_count = seq_count * span
    pos_all = jnp.arange(full_len, dtype=jnp.int32)
    hidden = inputs.reshape(row_count, width).astype(jnp.float32)
    attn_in_f, normed_one, scale_one = layer_norm(hidden, vector_f[0], vector_f[1])
    attn_in = attn_in_f.astype(jnp.bfloat16)
    projected = (jnp.dot(attn_in, w_qkv, preferred_element_type=jnp.float32) + bias_row).astype(
        jnp.bfloat16
    )
    queries = projected[:, :width].reshape(seq_count, span, width)
    key_value = projected[:, width:].reshape(seq_count, span, 2 * width)
    key_value_all = lax.all_gather(key_value, "replica", axis=1, tiled=True)
    offset = lax.axis_index("replica") * span
    pos_query = offset + jnp.arange(span, dtype=jnp.int32)
    seg_query = lax.dynamic_slice_in_dim(segments, offset, span, 1)

    def forward_one(element):
        return attend_forward(element[0], element[1], element[2], element[3], pos_query, pos_all)

    attended, log_norm = map_sequences(forward_one, (queries, key_value_all, seg_query, segments))
    attended_rows = attended.reshape(row_count, width)
    mixed = hidden + jnp.dot(attended_rows, w_out, preferred_element_type=jnp.float32) + vector_f[2]
    ffn_in_f, normed_two, scale_two = layer_norm(mixed, vector_f[3], vector_f[4])
    ffn_in = ffn_in_f.astype(jnp.bfloat16)
    pre_act = jnp.dot(ffn_in, w_fc, preferred_element_type=jnp.float32) + b_fc.astype(jnp.float32)
    activ, slope = gelu_parts(pre_act)
    activ_b = activ.astype(jnp.bfloat16)
    result = mixed + jnp.dot(activ_b, w_pr, preferred_element_type=jnp.float32) + vector_f[5]
    back_qkv, back_out, back_fc, back_pr, back_vec_f = (w_qkv, w_out, w_fc, w_pr, vector_f)
    cot_rows = cotangent.reshape(row_count, width)
    cot_f = cot_rows.astype(jnp.float32)
    grad_w_pr = jnp.dot(activ_b.T, cot_rows, preferred_element_type=jnp.float32)
    grad_b_pr = jnp.sum(cot_f, 0)
    grad_pre = jnp.dot(cot_rows, back_pr.T, preferred_element_type=jnp.float32) * slope
    grad_pre_b = grad_pre.astype(jnp.bfloat16)
    grad_w_fc = jnp.dot(ffn_in.T, grad_pre_b, preferred_element_type=jnp.float32)
    grad_b_fc = jnp.sum(grad_pre, 0)
    grad_ffn = jnp.dot(grad_pre_b, back_fc.T, preferred_element_type=jnp.float32)
    grad_gain_two = jnp.sum(grad_ffn * normed_two, 0)
    grad_bias_two = jnp.sum(grad_ffn, 0)
    grad_mixed = cot_f + norm_back(grad_ffn, back_vec_f[3], normed_two, scale_two)
    grad_mixed_b = grad_mixed.astype(jnp.bfloat16)
    grad_w_out = jnp.dot(attended_rows.T, grad_mixed_b, preferred_element_type=jnp.float32)
    grad_b_out = jnp.sum(grad_mixed, 0)
    grad_att = jnp.dot(grad_mixed_b, back_out.T, preferred_element_type=jnp.float32).astype(
        jnp.bfloat16
    )
    grad_att = grad_att.reshape(seq_count, span, width)

    def backward_one(element):
        return attend_backward(
            element[0],
            element[1],
            element[2],
            element[3],
            pos_query,
            pos_all,
            element[4],
            element[5],
            element[6],
        )

    grad_query, grad_kv_part = map_sequences(
        backward_one, (queries, key_value_all, seg_query, segments, log_norm, attended, grad_att)
    )
    grad_kv = lax.psum_scatter(
        grad_kv_part.astype(jnp.bfloat16), "replica", scatter_dimension=1, tiled=True
    ).astype(jnp.float32)
    grad_proj = jnp.concatenate([grad_query, grad_kv], 2).reshape(row_count, 3 * width)
    grad_proj_b = grad_proj.astype(jnp.bfloat16)
    grad_b_qkv = jnp.stack(
        [jnp.sum(grad_proj[:, :width], 0), jnp.sum(grad_proj[:, 2 * width :], 0)]
    )
    grad_w_qkv = jnp.dot(attn_in.T, grad_proj_b, preferred_element_type=jnp.float32)
    grad_in = jnp.dot(grad_proj_b, back_qkv.T, preferred_element_type=jnp.float32)
    grad_gain_one = jnp.sum(grad_in * normed_one, 0)
    grad_bias_one = jnp.sum(grad_in, 0)
    grad_input = grad_mixed + norm_back(grad_in, back_vec_f[0], normed_one, scale_one)
    grad_vec = jnp.stack(
        [grad_gain_one, grad_bias_one, grad_b_out, grad_gain_two, grad_bias_two, grad_b_pr]
    )
    groups = lax.axis_size("fsdp")
    small_grads = jnp.concatenate(
        [
            grad_vec.reshape(6, groups, shard).transpose(1, 0, 2),
            grad_b_qkv.reshape(2, groups, shard).transpose(1, 0, 2),
            grad_b_fc.reshape(groups, hidden_ratio, shard),
        ],
        1,
    )
    small_sums = lax.psum(small_grads, ("fsdp", "replica"))
    small_own = lax.dynamic_index_in_dim(small_sums, lax.axis_index("fsdp"), 0, keepdims=False)
    totals = (
        reduce_matrix(grad_w_qkv),
        small_own[6:8],
        reduce_matrix(grad_w_out),
        reduce_matrix(grad_w_fc),
        small_own[8:].reshape(-1),
        reduce_matrix(grad_w_pr),
        small_own[:6],
    )
    factor = float(row_count * lax.axis_size("fsdp") * lax.axis_size("replica")) ** (-0.5)
    grads = [total * factor for total in totals]
    new_w_qkv = adamw(w_qkv_state, grads[0], WEIGHT_DECAY)
    new_b_qkv = adamw(b_qkv_state, grads[1], 0.0)
    new_w_o = adamw(w_o_state, grads[2], WEIGHT_DECAY)
    new_w_fc = adamw(w_fc_state, grads[3], WEIGHT_DECAY)
    new_b_fc = adamw(b_fc_state, grads[4], 0.0)
    new_w_pr = adamw(w_pr_state, grads[5], WEIGHT_DECAY)
    new_vectors = adamw(vec_state, grads[6], 0.0)
    outputs = result.reshape(seq_count, span, width).astype(jnp.bfloat16)
    input_grad = grad_input.reshape(seq_count, span, width).astype(jnp.bfloat16)
    return (
        outputs,
        input_grad,
        grads[0],
        grads[1],
        grads[2],
        grads[3],
        grads[4],
        grads[5],
        grads[6],
        new_w_qkv,
        new_b_qkv,
        new_w_o,
        new_w_fc,
        new_b_fc,
        new_w_pr,
        new_vectors,
    )


def solution(mesh):
    in_specs = (
        P("fsdp", "replica", None),
        P("fsdp", "replica", None),
        P("fsdp", None),
        P(None, "fsdp", None),
        P(None, None, "fsdp"),
        P(None, "fsdp", None),
        P(None, "fsdp", None),
        P(None, "fsdp"),
        P(None, "fsdp", None),
        P(None, None, "fsdp"),
    )
    out_specs = (
        P("fsdp", "replica", None),
        P("fsdp", "replica", None),
        P("fsdp", None),
        P(None, "fsdp"),
        P("fsdp", None),
        P("fsdp", None),
        P("fsdp"),
        P("fsdp", None),
        P(None, "fsdp"),
        P(None, "fsdp", None),
        P(None, None, "fsdp"),
        P(None, "fsdp", None),
        P(None, "fsdp", None),
        P(None, "fsdp"),
        P(None, "fsdp", None),
        P(None, None, "fsdp"),
    )
    return jax.shard_map(body, mesh=mesh, in_specs=in_specs, out_specs=out_specs, check_vma=False)
```
